128 devices in a mesh: gx: 16 (over z, y_lo, core), gy: 8 (over y_hi, x).
Axes of the slice: x: 4, y: 4 (y_hi: 2, y_lo: 2; y = y_hi * 2 + y_lo), z: 4, core: 2. Of those that a mesh axis runs over, the one named last changes fastest.
Arguments:
- electric: float32 [3, 1024, 256, 128], P(None, 'gx', 'gy'), may hold values from -6 to 6
- magnetic: float32 [3, 1024, 256, 128], P(None, 'gx', 'gy'), may hold values from -6 to 6
- material_ids: int32 [1024, 256, 128], P('gx', 'gy'), may hold values from 0 to 7
- inv_permittivity: float32 [8], replicated, may hold values from 0.08 to 1
- forward_field: bfloat16 [3, 3, 1024, 256, 128], P(None, None, 'gx', 'gy'), may hold values from -6 to 6
- source_values: float32 [65536, 384], P(('gx', 'gy')), may hold values from -6 to 6
- source_tile: int32 [65536, 1], P(('gx', 'gy')), may hold values from 0 to 127; in each aligned block of 512 rows (0 to 511, 512 to 1023, ...) at most 8 rows name the same one
- source_cell: int32 [65536], P(('gx', 'gy')), may hold values from 0 to 2047
- owner_map: int32 [64], replicated, may hold values from 0 to 127, as said below
- shape_basis: float32 [128, 64, 64], replicated, may hold values from -0.09375 to 0.09375
Outputs:
- adjoint_e: float32 [3, 1024, 256, 128], P(None, 'gx', 'gy')
- adjoint_h: float32 [3, 1024, 256, 128], P(None, 'gx', 'gy')
- design_gradient: float32 [128, 128], P(('gx', 'gy'))
The draws below stay inside these ranges and needn't reach their ends.
Inputs may be any that keep to these rules, and one draw needn't show every extreme that they name: `source_tile`: each device's 512 source blocks name any one tile at most 8 times, a bound that some block reaches. `owner_map`: the owners of different design blocks are different devices; device 0 and the last device each own one.
All inputs are finite; a program needn't handle non-finite values.
Results may differ from the reference program's by a relative error of at most 0.0003.
Values sent between devices are 32-bit elements; how exact they have to be, the bound alone decides.
No kernel may reach another device: no remote copies, remote signals or barrier semaphores. Data moves between devices by JAX's collectives and lax.ppermute only.
A program may use at most 128 MiB of HBM per device.

```python
import math
import jax
import jax.numpy as jnp
import numpy as np
from jax import lax

CX = 64
CY = 32
NZ = 128
STEPS = 3
MATERIALS = 8
BLOCK = 64
PARAMS = 128
SRC_DEV = 512
NX = 1024
NY = 256
CAP = 8
BLOCKS_ALL = 65536
DESIGN_BLOCKS = 64
N_GX = 16
N_GY = 8
DEVICES = 128


def draw_owner_map(key, part):
    first_key = jax.random.fold_in(key, 11)
    second_key = jax.random.fold_in(key, 23)
    middle = jax.random.permutation(first_key, N_GX * N_GY - 2) + 1
    ends = jnp.array([0, N_GX * N_GY - 1], jnp.int32)
    chosen = jnp.concatenate([ends, middle[:DESIGN_BLOCKS - 2].astype(jnp.int32)])
    return jax.random.permutation(second_key, chosen).astype(jnp.int32)


def touch_ends(values, own_key, low, largest):
    longest = values.shape.index(max(values.shape))
    spots = []
    for shift in (0, 1):
        where = [jax.random.randint(jax.random.fold_in(own_key, axis), (), 0, length) for axis, length in enumerate(values.shape)]
        where[longest] = (where[longest] + shift) % values.shape[longest]
        spots.append(tuple(where))
    return values.at[spots[0]].set(low).at[spots[1]].set(largest)


def shard_levels(rng, extent, split, low, high):
    def one(position, blocks):
        steps = jax.random.uniform(jax.random.fold_in(jax.random.fold_in(rng, 6), position), (blocks,), jnp.float32, low / len(split), high / len(split))
        return jnp.repeat(jnp.exp(steps), extent[position] // blocks).reshape((-1,) + (1,) * (len(extent) - position - 1))

    level = one(*split[0])
    for cut in split[1:]:
        level = level * one(*cut)
    return level


def assign_block(stream_key, own, number, rows, amount, top, bound, slope):
    sequence = jax.random.permutation(stream_key, amount)
    heavy_load, usual = shares(amount, rows * top, bound, slope, True), shares(amount, rows * top, bound, slope, False)
    places = jnp.arange(amount)

    def named(tallies, offset_by):
        used = int((tallies > 0).sum())
        fixed = max(1, used // 4)
        shifted = fixed + (places - fixed + offset_by * (used - fixed)) % max(1, amount - fixed)
        return jnp.zeros((amount,), jnp.int32).at[sequence[jnp.where(places < fixed, places, shifted)]].set(jnp.asarray(tallies, jnp.int32))

    tallies = jnp.where(number % 4 == 0, named(heavy_load, number // 4), named(usual, number - number // 4 - 1))
    mixed = jax.random.permutation(jax.random.fold_in(own, 3), amount)
    donor, receiver = mixed[0:amount // 2 * 2:2], mixed[1:amount // 2 * 2:2]
    margin = jnp.minimum(tallies[donor] - 1, bound - tallies[receiver]) // 2
    margin = jnp.where((donor == sequence[0]) | (receiver == sequence[0]) | (tallies[receiver] == 0), 0, jnp.maximum(margin, 0))
    shifted = jax.random.randint(jax.random.fold_in(own, 4), (amount // 2,), 0, 1 << 20) % (margin + 1)
    tallies = tallies.at[donor].add(-shifted).at[receiver].add(shifted)
    members = jnp.searchsorted(jnp.cumsum(tallies), jnp.arange(rows * top), side="right").astype(jnp.int32)
    listing = members.reshape(top, rows).T
    listing = listing[jax.random.permutation(jax.random.fold_in(own, 1), rows)]
    offset_by = jax.random.randint(jax.random.fold_in(own, 2), (rows, 1), 0, top)
    return jnp.take_along_axis(listing, (jnp.arange(top)[None, :] + offset_by) % top, axis=1)


def shares(count, total, limit, skew, full):
    loads = [(1 << 20) // math.isqrt(grade ** skew) + 1 for grade in range(1, count + 1)]
    largest = limit if full else min(limit, max(-(-total // count), total * loads[0] // sum(loads)))
    least = 1 if total - largest >= count - 1 else 0
    given, spare = [largest] + [least] * (count - 1), total - largest - least * (count - 1)
    while spare > 0:
        free = [i for i in range(1, count) if given[i] < largest] or [i for i in range(1, count) if given[i] < limit]
        whole, budget = sum([loads[i] for i in free]), spare
        for i in free:
            addition = min(limit - given[i], max(1, budget * loads[i] // whole), spare)
            given[i] = given[i] + addition
            spare = spare - addition
    return np.array(given)


def normal_values(own_key, dims, spread, reach, cuts=(), kind=jnp.bfloat16):
    entries = spread * jax.random.normal(own_key, dims, jnp.float32)
    if cuts:
        entries = entries * shard_levels(own_key, dims, cuts, -0.22, 0.18)
    return jnp.clip(entries, -reach, reach).astype(kind)


def setup_inputs(seed: int = 0) -> dict:
    key_of = jax.random.split(jax.random.key(seed), 11)
    electric = normal_values(key_of[0], (3, NX, NY, NZ), 1.0, 6.0, ((1, 16), (2, 8)), jnp.float32)
    magnetic = normal_values(key_of[1], (3, NX, NY, NZ), 1.0, 6.0, ((1, 16), (2, 8)), jnp.float32)
    material_ids = touch_ends(jax.random.randint(key_of[2], (NX, NY, NZ), 0, MATERIALS), jax.random.fold_in(key_of[2], 1), 0, MATERIALS - 1).astype(jnp.int32)
    inv_permittivity = jnp.clip(jnp.exp(jax.random.uniform(key_of[3], (MATERIALS,), jnp.float32, math.log(0.08), math.log(1.0))), 0.08, 1.0)
    forward_field = normal_values(key_of[4], (STEPS, 3, NX, NY, NZ), 1.0, 6.0, ((2, 16), (3, 8)))
    source_values = normal_values(key_of[5], (BLOCKS_ALL, STEPS * NZ), 1.0, 6.0, ((0, 128),), jnp.float32)
    source_tile_keys = jax.random.split(jax.random.fold_in(key_of[6], 1), BLOCKS_ALL // SRC_DEV)
    source_tile_turns = jax.random.permutation(jax.random.fold_in(key_of[6], 3), BLOCKS_ALL // SRC_DEV)
    source_tile = jax.vmap(lambda own, number: assign_block(jax.random.fold_in(key_of[6], 2), own, number, SRC_DEV, DEVICES, 1, CAP, 2))(source_tile_keys, source_tile_turns).reshape((BLOCKS_ALL, 1))
    source_cell = touch_ends(jax.random.randint(key_of[7], (BLOCKS_ALL,), 0, CX * CY), jax.random.fold_in(key_of[7], 1), 0, (CX * CY) - 1).astype(jnp.int32)
    owner_map = draw_owner_map(jax.random.fold_in(key_of[10], 71), 0)
    shape_basis = normal_values(key_of[9], (PARAMS, BLOCK, BLOCK), (BLOCK * BLOCK) ** -0.5, 0.09375, (), jnp.float32)
    return {"electric": electric, "magnetic": magnetic, "material_ids": material_ids, "inv_permittivity": inv_permittivity, "forward_field": forward_field, "source_values": source_values, "source_tile": source_tile, "source_cell": source_cell, "owner_map": owner_map, "shape_basis": shape_basis}


time_step = 0.5
corr_scale = 0.0625


def plus_one(a, axis):
    rest = lax.slice_in_dim(a, 1, a.shape[axis], axis=axis)
    edge = jnp.zeros_like(lax.slice_in_dim(a, 0, 1, axis=axis))
    return jnp.concatenate([rest, edge], axis=axis)


def minus_one(a, axis):
    rest = lax.slice_in_dim(a, 0, a.shape[axis] - 1, axis=axis)
    edge = jnp.zeros_like(lax.slice_in_dim(a, 0, 1, axis=axis))
    return jnp.concatenate([edge, rest], axis=axis)


def reference(electric, magnetic, material_ids, inv_permittivity, forward_field, source_values, source_tile, source_cell, owner_map, shape_basis):
    inv_eps = jnp.zeros(material_ids.shape, jnp.float32)
    for mat in range(MATERIALS):
        inv_eps = inv_eps + jnp.where(material_ids == mat, inv_permittivity[mat], jnp.zeros((), inv_permittivity.dtype))
    target = source_tile[:, 0]
    col_x = (target // N_GY) * CX + source_cell // CY
    col_y = (target % N_GY) * CY + source_cell % CY
    corr = jnp.zeros((NX, NY), jnp.float32)
    for step in range(STEPS):
        ex, ey, ez = electric[0], electric[1], electric[2]
        curl_x = (plus_one(ez, 1) - ez) - (plus_one(ey, 2) - ey)
        curl_y = (plus_one(ex, 2) - ex) - (plus_one(ez, 0) - ez)
        curl_z = (plus_one(ey, 0) - ey) - (plus_one(ex, 1) - ex)
        magnetic = magnetic - time_step * jnp.stack([curl_x, curl_y, curl_z])
        hx, hy, hz = magnetic[0], magnetic[1], magnetic[2]
        drive = jnp.zeros((NX, NY, NZ), jnp.float32).at[col_x, col_y].add(source_values[:, step * NZ:(step + 1) * NZ])
        back_x = (hz - minus_one(hz, 1)) - (hy - minus_one(hy, 2))
        back_y = (hx - minus_one(hx, 2)) - (hz - minus_one(hz, 0))
        back_z = (hy - minus_one(hy, 0)) - (hx - minus_one(hx, 1)) - drive
        electric = electric + time_step * inv_eps * jnp.stack([back_x, back_y, back_z])
        corr = corr + jnp.sum(forward_field[step].astype(jnp.float32) * electric, axis=(0, 3))
    corr = corr * corr_scale
    blocks = corr.reshape(NX // BLOCK, BLOCK, NY // BLOCK, BLOCK).transpose(0, 2, 1, 3).reshape(DESIGN_BLOCKS, BLOCK * BLOCK)
    grads = jnp.dot(blocks, shape_basis.reshape(PARAMS, BLOCK * BLOCK).T, preferred_element_type=jnp.float32, precision=lax.Precision.HIGHEST)
    design_gradient = jnp.zeros((N_GX * N_GY, PARAMS), jnp.float32).at[owner_map].set(grads)
    return electric, magnetic, design_gradient
```

```python
import jax
import jax.numpy as jnp
from jax import lax
from jax.sharding import PartitionSpec as P

time_step = 0.5
corr_scale = 0.0625


def shifted(value, axis, steps):
    count = lax.axis_size(axis)
    leading, last = (max(0, -steps), min(count, count - steps))
    return lax.ppermute(value, axis, [(source, source + steps) for source in range(leading, last)])


def z_plus(field):
    return jnp.concatenate([field[:, :, 1:], jnp.zeros_like(field[:, :, :1])], axis=2)


def z_minus(field):
    return jnp.concatenate([jnp.zeros_like(field[:, :, :1]), field[:, :, :-1]], axis=2)


def per_device(
    electric,
    magnetic,
    material_ids,
    inv_permittivity,
    forward_field,
    source_values,
    source_tile,
    source_cell,
    owner_map,
    shape_basis,
):
    width_x = electric.shape[1]
    width_y = electric.shape[2]
    depth = electric.shape[3]
    steps = forward_field.shape[0]
    grid_x = lax.axis_size("gx")
    grid_y = lax.axis_size("gy")
    devices = grid_x * grid_y
    index_x = lax.axis_index("gx")
    index_y = lax.axis_index("gy")
    inv_eps = jnp.zeros(material_ids.shape, jnp.float32)
    for mat in range(inv_permittivity.shape[0]):
        inv_eps = inv_eps + jnp.where(material_ids == mat, inv_permittivity[mat], jnp.float32(0.0))
    count = source_tile.shape[0]
    capacity = max(2, 2 * count // devices)
    target = source_tile[:, 0]
    order = jnp.arange(count, dtype=jnp.int32)
    same = target[:, None] == target[None, :]
    earlier = order[None, :] < order[:, None]
    slot = jnp.sum((same & earlier).astype(jnp.int32), axis=1)
    dest_row = target * capacity + slot
    packed = (
        jnp.zeros((devices * capacity, source_values.shape[1]), jnp.float32)
        .at[dest_row]
        .set(source_values)
    )
    packed_cells = (
        jnp.full((devices * capacity,), -1.0, jnp.float32)
        .at[dest_row]
        .set(source_cell.astype(jnp.float32))
    )
    got_values, got_cells = (
        lax.all_to_all(
            packed.reshape(devices, capacity, -1),
            ("gx", "gy"),
            split_axis=0,
            concat_axis=0,
            tiled=True,
        ),
        lax.all_to_all(
            packed_cells.reshape(devices, capacity),
            ("gx", "gy"),
            split_axis=0,
            concat_axis=0,
            tiled=True,
        ),
    )
    got_values = got_values.reshape(devices * capacity, -1)
    got_cells = got_cells.reshape(devices * capacity).astype(jnp.int32)
    cell_total = width_x * width_y
    safe_cells = jnp.where(got_cells < 0, cell_total, got_cells)
    drive = (
        jnp.zeros((cell_total, got_values.shape[1]), jnp.float32)
        .at[safe_cells]
        .add(got_values, mode="drop")
    )
    drive = drive.reshape(width_x, width_y, steps, depth)
    corr = jnp.zeros((width_x, width_y), jnp.float32)
    for step in range(steps):
        ex, ey, ez = (electric[0], electric[1], electric[2])
        face_x = shifted(electric[1:3, 0], "gx", -1)
        face_y = shifted(jnp.stack([ex[:, 0], ez[:, 0]]), "gy", -1)
        ey_next_x = jnp.concatenate([ey[1:], face_x[0][None]], axis=0)
        ez_next_x = jnp.concatenate([ez[1:], face_x[1][None]], axis=0)
        ex_next_y = jnp.concatenate([ex[:, 1:], face_y[0][:, None]], axis=1)
        ez_next_y = jnp.concatenate([ez[:, 1:], face_y[1][:, None]], axis=1)
        curl_x = ez_next_y - ez - (z_plus(ey) - ey)
        curl_y = z_plus(ex) - ex - (ez_next_x - ez)
        curl_z = ey_next_x - ey - (ex_next_y - ex)
        magnetic = magnetic - time_step * jnp.stack([curl_x, curl_y, curl_z])
        hx, hy, hz = (magnetic[0], magnetic[1], magnetic[2])
        rim_x = shifted(magnetic[1:3, -1], "gx", 1)
        rim_y = shifted(jnp.stack([hx[:, -1], hz[:, -1]]), "gy", 1)
        hy_prev_x = jnp.concatenate([rim_x[0][None], hy[:-1]], axis=0)
        hz_prev_x = jnp.concatenate([rim_x[1][None], hz[:-1]], axis=0)
        hx_prev_y = jnp.concatenate([rim_y[0][:, None], hx[:, :-1]], axis=1)
        hz_prev_y = jnp.concatenate([rim_y[1][:, None], hz[:, :-1]], axis=1)
        back_x = hz - hz_prev_y - (hy - z_minus(hy))
        back_y = hx - z_minus(hx) - (hz - hz_prev_x)
        back_z = hy - hy_prev_x - (hx - hx_prev_y) - drive[:, :, step]
        electric = electric + time_step * inv_eps * jnp.stack([back_x, back_y, back_z])
        corr = corr + jnp.sum(forward_field[step].astype(jnp.float32) * electric, axis=(0, 3))
    corr = corr * corr_scale
    block_side = shape_basis.shape[1]
    params = shape_basis.shape[0]
    start_x = index_x * width_x
    start_y = index_y * width_y
    design_block = start_x // block_side * (width_y * grid_y // block_side) + start_y // block_side
    window = lax.dynamic_slice(
        shape_basis,
        (jnp.int32(0), start_x % block_side, start_y % block_side),
        (params, width_x, width_y),
    )
    partial_grad = jnp.dot(
        window.reshape(params, width_x * width_y),
        corr.reshape(width_x * width_y),
        preferred_element_type=jnp.float32,
        precision=lax.Precision.HIGHEST,
    )
    block_ids = jnp.arange(owner_map.shape[0], dtype=jnp.int32)
    owner = jnp.sum(jnp.where(block_ids == design_block, owner_map, 0))
    device_ids = jnp.arange(devices, dtype=jnp.int32)
    rows = jnp.where(device_ids[:, None] == owner, partial_grad[None, :], jnp.float32(0.0))
    got_rows = lax.all_to_all(rows, ("gx", "gy"), split_axis=0, concat_axis=0, tiled=True)
    design_gradient = jnp.sum(got_rows, axis=0, keepdims=True)
    return (electric, magnetic, design_gradient)


def solution(mesh):
    placed = (
        P(None, "gx", "gy", None),
        P(None, "gx", "gy", None),
        P("gx", "gy", None),
        P(),
        P(None, None, "gx", "gy", None),
        P(("gx", "gy"), None),
        P(("gx", "gy"), None),
        P(("gx", "gy")),
        P(),
        P(),
    )
    return jax.shard_map(
        per_device,
        mesh=mesh,
        in_specs=placed,
        out_specs=(P(None, "gx", "gy", None), P(None, "gx", "gy", None), P(("gx", "gy"), None)),
        check_vma=False,
    )
```
